32 devices in a mesh: grp: 8 (over y, x, core), seq: 4 (over z).
Axes of the slice: x: 2, y: 2, z: 4, core: 2. Of those that a mesh axis runs over, the one named last changes fastest.
Arguments:
- tokens: bfloat16 [16384, 1024], P(('grp', 'seq')), may hold values from -6 to 6
- cotangent: bfloat16 [16384, 1024], P(('grp', 'seq')), may hold values from -6 to 6
- image_of_token: int32 [16384], P('grp'), may hold values from 0 to 3, as said below
- ln1_gain: bfloat16 [1024], P(('grp', 'seq')), may hold values from 0.5 to 1.5
- ln1_bias: bfloat16 [1024], P(('grp', 'seq')), may hold values from -2 to 2
- qkv_weight: bfloat16 [1024, 3072], P(('grp', 'seq')), may hold values from -0.1875 to 0.1875
- q_bias: bfloat16 [1024], P(('grp', 'seq')), may hold values from -2 to 2
- v_bias: bfloat16 [1024], P(('grp', 'seq')), may hold values from -2 to 2
- out_weight: bfloat16 [1024, 1024], P(('grp', 'seq')), may hold values from -0.75 to 0.75
- out_bias: bfloat16 [1024], P(('grp', 'seq')), may hold values from -2 to 2
- ln2_gain: bfloat16 [1024], P(('grp', 'seq')), may hold values from 0.5 to 1.5
- ln2_bias: bfloat16 [1024], P(('grp', 'seq')), may hold values from -2 to 2
- up_weight: bfloat16 [1024, 4096], P(('grp', 'seq')), may hold values from -0.1875 to 0.1875
- up_bias: bfloat16 [4096], P(('grp', 'seq')), may hold values from -3 to 3
- down_weight: bfloat16 [4096, 1024], P(('grp', 'seq')), may hold values from -0.09375 to 0.09375
- down_bias: bfloat16 [1024], P(('grp', 'seq')), may hold values from -2 to 2
Outputs:
- output: bfloat16 [16384, 1024], P(('grp', 'seq'))
- input_grad: bfloat16 [16384, 1024], P(('grp', 'seq'))
- ln1_gain_grad: float32 [1024], P(('grp', 'seq'))
- ln1_bias_grad: float32 [1024], P(('grp', 'seq'))
- qkv_weight_grad: float32 [1024, 3072], P(('grp', 'seq'))
- q_bias_grad: float32 [1024], P(('grp', 'seq'))
- v_bias_grad: float32 [1024], P(('grp', 'seq'))
- out_weight_grad: float32 [1024, 1024], P(('grp', 'seq'))
- out_bias_grad: float32 [1024], P(('grp', 'seq'))
- ln2_gain_grad: float32 [1024], P(('grp', 'seq'))
- ln2_bias_grad: float32 [1024], P(('grp', 'seq'))
- up_weight_grad: float32 [1024, 4096], P(('grp', 'seq'))
- up_bias_grad: float32 [4096], P(('grp', 'seq'))
- down_weight_grad: float32 [4096, 1024], P(('grp', 'seq'))
- down_bias_grad: float32 [1024], P(('grp', 'seq'))
The draws below stay inside these ranges and needn't reach their ends.
Inputs may be any that keep to these rules, and one draw needn't show every extreme that they name: `image_of_token`: each group of 2048 slots (one index of grp) holds 1 to 3 whole images of 577 tokens, numbered 0, 1, ... from its first slot; the rest of its slots are marked 3 and attend to one another; some group holds 3 images.
All inputs are finite; a program needn't handle non-finite values.
Results may differ from the reference program's by a relative error of at most 0.012.
Values may be sent and summed in bfloat16 or wider, within the bound.
A program may use at most 192 MiB of HBM per device.

```python
import math
import jax
import jax.numpy as jnp
from jax import lax

D = 1024
HEADS = 16
HEAD_DIM = 64
FF = 4096
IMG_LEN = 577
GROUPS = 8
GROUP_TOK = 2048
TOKENS = 16384
IMGS_MAX = 3


def draw_image_of_token(key, part):
    count_key = jax.random.fold_in(key, 11)
    fullest_key = jax.random.fold_in(key, 12)
    counts = jax.random.randint(count_key, (GROUPS,), 1, IMGS_MAX + 1)
    fullest = jax.random.randint(fullest_key, (), 0, GROUPS)
    counts = jnp.where(jnp.arange(GROUPS) == fullest, IMGS_MAX, counts)
    image = jnp.arange(GROUP_TOK) // IMG_LEN
    labels = jnp.where(image[None, :] < counts[:, None], image[None, :], IMGS_MAX)
    return labels.reshape(TOKENS).astype(jnp.int32)


def with_spikes(values, own_key, source, target, shards_of, factor):
    owner, partner = [(jnp.arange(values.shape[axis_at]) // (values.shape[axis_at] // shards_of)).reshape([-1 if axis == axis_at else 1 for axis in range(values.ndim)]) for axis_at in (source, target)]
    chosen = jax.random.permutation(own_key, shards_of)[partner]
    strong = (owner == chosen) | (owner == (partner + shards_of // 2) % shards_of)
    return jnp.where(strong, factor * values, values)


def levels(key, dims, pieces, least, high):
    level = 1.0
    for axis_at, shards_of in pieces:
        heights = jax.random.uniform(jax.random.fold_in(jax.random.fold_in(key, 6), axis_at), (shards_of,), jnp.float32, least / len(pieces), high / len(pieces))
        level = level * jnp.repeat(jnp.exp(heights), dims[axis_at] // shards_of).reshape((-1,) + (1,) * (len(dims) - 1 - axis_at))
    return level


def noise(own_key, dims, scale, most, cuts=(), dtype=jnp.bfloat16):
    values = jax.random.normal(own_key, dims, jnp.float32) * scale
    if len(cuts) > 0:
        values = levels(own_key, dims, cuts, -0.22, 0.18) * values
    return jnp.clip(values, min=-most, max=most).astype(dtype)


def noise_with(own_key, shape, scale, most, split, heavy, kind=jnp.bfloat16):
    values = scale * jax.random.normal(own_key, shape, jnp.float32)
    if split:
        values = values * levels(own_key, shape, split, -0.22, 0.18)
    return jnp.clip(with_spikes(values, jax.random.fold_in(own_key, 3), *heavy), -most, most).astype(kind)


def setup_inputs(seed: int = 0) -> dict:
    key_of = jax.random.split(jax.random.key(seed), 17)
    return {
        "tokens": noise(key_of[0], (TOKENS, D), 1.0, 6.0, ((0, 32),)),
        "cotangent": noise_with(key_of[1], (TOKENS, D), 1.0, 6.0, ((0, 32),), (0, 1, 32, 2.75)),
        "image_of_token": draw_image_of_token(jax.random.fold_in(key_of[16], 71), 0),
        "ln1_gain": jnp.clip(1.0 + 0.1 * jax.random.normal(key_of[3], (D,), jnp.float32), 0.5, 1.5).astype(jnp.bfloat16),
        "ln1_bias": noise(key_of[4], (D,), 0.3, 2.0, ((0, 32),)),
        "qkv_weight": noise(key_of[5], (D, 3 * D), D ** -0.5, 0.1875, ((0, 32),)),
        "q_bias": noise(key_of[6], (D,), 0.3, 2.0, ((0, 32),)),
        "v_bias": noise(key_of[7], (D,), 0.3, 2.0, ((0, 32),)),
        "out_weight": noise(key_of[8], (D, D), (D // 16) ** -0.5, 0.75, ((0, 32),)),
        "out_bias": noise(key_of[9], (D,), 0.3, 2.0, ((0, 32),)),
        "ln2_gain": jnp.clip(1.0 + 0.1 * jax.random.normal(key_of[10], (D,), jnp.float32), 0.5, 1.5).astype(jnp.bfloat16),
        "ln2_bias": noise(key_of[11], (D,), 0.3, 2.0, ((0, 32),)),
        "up_weight": noise(key_of[12], (D, FF), D ** -0.5, 0.1875, ((0, 32),)),
        "up_bias": noise(key_of[13], (FF,), 0.5, 3.0, ((0, 32),)),
        "down_weight": noise(key_of[14], (FF, D), FF ** -0.5, 0.09375, ((0, 32),)),
        "down_bias": noise(key_of[15], (D,), 0.3, 2.0, ((0, 32),)),
    }


@jax.custom_vjp
def low(v):
    return lax.optimization_barrier(v.astype(jnp.bfloat16)).astype(jnp.float32)

@jax.custom_vjp
def low_back(v):
    return v

def low_keep(v):
    return (low(v), None)

def low_pass(kept, grad):
    return (grad,)

def back_keep(v):
    return (v, None)

def back_low(kept, grad):
    return (low(grad),)
low.defvjp(low_keep, low_pass)
low_back.defvjp(back_keep, back_low)
EPS = 1e-06
MASKED = -1e+30
HIGH = lax.Precision.HIGHEST

def matmul(left, right):
    return jnp.dot(left, right, precision=HIGH, preferred_element_type=jnp.float32)

def layer_norm(value, gain, shift):
    center = value - lax.optimization_barrier(jnp.mean(value, axis=-1, keepdims=True))
    spread = lax.optimization_barrier(jnp.mean(center * center, axis=-1, keepdims=True))
    return center * lax.rsqrt(spread + EPS) * gain + shift

def head_attention(item):
    query, key_rows, value_rows, labels = item
    same = labels[:, None] == labels[None, :]
    scale = 1.0 / math.sqrt(query.shape[-1])
    scores = low_back(jnp.where(same, matmul(query, key_rows.T) * scale, MASKED))
    probs = low(jax.nn.softmax(scores, axis=-1))
    return matmul(probs, value_rows)

def to_items(rows, groups):
    return rows.reshape(groups, GROUP_TOK, HEADS, HEAD_DIM).transpose(0, 2, 1, 3).reshape(groups * HEADS, GROUP_TOK, HEAD_DIM)

def forward(inputs, labels, ln1_gain, ln1_bias, qkv_weight, q_bias, v_bias, out_weight, out_bias, ln2_gain, ln2_bias, up_weight, up_bias, down_weight, down_bias):
    groups = inputs.shape[0] // GROUP_TOK
    normed1 = low(layer_norm(inputs, ln1_gain, ln1_bias))
    zeros = jnp.zeros_like(q_bias)
    joint = low(low_back(matmul(normed1, qkv_weight) + jnp.concatenate([q_bias, zeros, v_bias])))
    queries = to_items(joint[:, :D], groups)
    keys = to_items(joint[:, D:2 * D], groups)
    values = to_items(joint[:, 2 * D:], groups)
    label_items = jnp.repeat(labels.reshape(groups, GROUP_TOK), HEADS, axis=0)
    heads_out = lax.map(jax.checkpoint(head_attention), (queries, keys, values, label_items))
    merged = heads_out.reshape(groups, HEADS, GROUP_TOK, HEAD_DIM).transpose(0, 2, 1, 3).reshape(groups * GROUP_TOK, D)
    attended = low(low_back(merged))
    resid = inputs + low_back(matmul(attended, out_weight) + out_bias)
    normed2 = low(layer_norm(resid, ln2_gain, ln2_bias))
    hidden = low_back(matmul(normed2, up_weight) + up_bias)
    active = low(jax.nn.gelu(hidden, approximate=False))
    return resid + matmul(active, down_weight) + down_bias

def reference(tokens, cotangent, image_of_token, ln1_gain, ln1_bias, qkv_weight, q_bias, v_bias, out_weight, out_bias, ln2_gain, ln2_bias, up_weight, up_bias, down_weight, down_bias):
    params = [p.astype(jnp.float32) for p in (ln1_gain, ln1_bias, qkv_weight, q_bias, v_bias, out_weight, out_bias, ln2_gain, ln2_bias, up_weight, up_bias, down_weight, down_bias)]
    inputs = tokens.astype(jnp.float32)

    def wrapped(value, *weights):
        return forward(value, image_of_token, *weights)
    result, pullback = jax.vjp(wrapped, inputs, *params)
    grads = pullback(cotangent.astype(jnp.float32))
    return (result.astype(jnp.bfloat16), grads[0].astype(jnp.bfloat16), grads[1], grads[2], grads[3], grads[4], grads[5], grads[6], grads[7], grads[8], grads[9], grads[10], grads[11], grads[12], grads[13])
```

```python
from functools import partial
import math

import jax
import jax.numpy as jnp
from jax import lax
from jax.experimental import pallas as pl
from jax.experimental.pallas import tpu as pltpu
from jax.sharding import PartitionSpec as P

HEADS = 16


EPS = 1e-06
MASKED = -1e30


def layer_norm(value, gain, shift):
    center = value - jnp.mean(value, axis=-1, keepdims=True)
    spread = jnp.mean(center * center, axis=-1, keepdims=True)
    return center * lax.rsqrt(spread + EPS) * gain + shift


def scaled_norm(value, gain):
    return layer_norm(value, gain, 0.0)


def rows_dot(left, right):
    return lax.dot_general(
        left, right, (((0,), (0,)), ((), ())), preferred_element_type=jnp.float32
    )


def dot_back(left, right):
    return lax.dot_general(
        left, right, (((1,), (1,)), ((), ())), preferred_element_type=jnp.float32
    )


BLOCK = 256


def head_lanes(shape, head, size):
    lane = lax.broadcasted_iota(jnp.int32, shape, len(shape) - 1)
    return lane // size == head


def forward_kernel(heads, first_ref, last_ref, q_ref, kv_ref, row_ref, col_ref, out_ref, lse_ref, s_ref):
    step = pl.program_id(0)
    first = first_ref[step]
    last = last_ref[step]
    width = q_ref.shape[1]
    size = width // heads
    query = q_ref[...] * (1.0 / math.sqrt(size))
    mine = row_ref[...]
    for head in range(heads):
        own = jnp.where(head_lanes(query.shape, head, size), query, jnp.zeros_like(query))

        def scores_at(at, peak):
            rows = pl.ds(pl.multiple_of(at * BLOCK, BLOCK), BLOCK)
            scores = lax.dot_general(
                own,
                kv_ref[rows, :width],
                (((1,), (1,)), ((), ())),
                preferred_element_type=jnp.float32,
            )
            scores = jnp.where(mine == col_ref[at], scores, MASKED)
            s_ref[head, at] = scores
            return jnp.maximum(peak, scores)

        peak = lax.fori_loop(first, last, scores_at, jnp.full((BLOCK, BLOCK), MASKED, jnp.float32))
        peak = jnp.max(peak, axis=-1, keepdims=True)

        def sum_at(at, carry):
            total, result = carry
            rows = pl.ds(pl.multiple_of(at * BLOCK, BLOCK), BLOCK)
            expo = jnp.exp(s_ref[head, at] - peak)
            result = result + jnp.dot(
                expo.astype(jnp.bfloat16),
                kv_ref[rows, width:],
                preferred_element_type=jnp.float32,
            )
            return (total + expo, result)

        total, result = lax.fori_loop(
            first,
            last,
            sum_at,
            (jnp.zeros((BLOCK, BLOCK), jnp.float32), jnp.zeros((BLOCK, width), jnp.float32)),
        )
        total = jnp.sum(total, axis=-1, keepdims=True)
        result = result / total
        lse_ref[:, head : head + 1] = peak + jnp.log(total)
        if head == 0:
            merged = result
        else:
            merged = jnp.where(head_lanes(result.shape, head, size), result, merged)
    out_ref[...] = merged.astype(out_ref.dtype)


def backward_kernel(
    heads, first_ref, last_ref, q_ref, kv_ref, g_ref, lse_ref, delta_ref, row_ref, col_ref,
    dq_ref, dkv_ref, sum_ref
):
    step = pl.program_id(0)
    first = first_ref[step]
    last = last_ref[step]
    width = q_ref.shape[1]
    size = width // heads
    scale = 1.0 / math.sqrt(size)

    @pl.when(step == 0)
    def clear():
        sum_ref[...] = jnp.zeros_like(sum_ref)

    keys = kv_ref[:, :width] * scale
    values = kv_ref[:, width:]
    mine = row_ref[...]
    for head in range(heads):
        lanes = head_lanes(keys.shape, head, size)
        own_keys = jnp.where(lanes, keys, jnp.zeros_like(keys))
        own_values = jnp.where(lanes, values, jnp.zeros_like(values))

        def at_queries(at, carry):
            grad_keys, grad_values = carry
            rows = pl.ds(pl.multiple_of(at * BLOCK, BLOCK), BLOCK)
            query = q_ref[rows, :]
            grad = g_ref[rows, :]
            scores = lax.dot_general(
                own_keys, query, (((1,), (1,)), ((), ())), preferred_element_type=jnp.float32
            )
            scores = jnp.where(mine == col_ref[at], scores, MASKED)
            weights = jnp.exp(scores - lse_ref[at, head : head + 1, :])
            grad_probs = lax.dot_general(
                own_values, grad, (((1,), (1,)), ((), ())), preferred_element_type=jnp.float32
            )
            grad_scores = (weights * (grad_probs - delta_ref[at, head : head + 1, :])).astype(
                jnp.bfloat16
            )
            grad_values = grad_values + jnp.dot(
                weights.astype(jnp.bfloat16), grad, preferred_element_type=jnp.float32
            )
            grad_keys = grad_keys + jnp.dot(
                grad_scores, query, preferred_element_type=jnp.float32
            )
            sum_ref[rows, :] += rows_dot(grad_scores, own_keys)
            return (grad_keys, grad_values)

        zero = jnp.zeros((BLOCK, width), jnp.float32)
        grad_keys, grad_values = lax.fori_loop(first, last, at_queries, (zero, zero))
        if head == 0:
            merged_keys, merged_values = grad_keys, grad_values
        else:
            merged_keys = jnp.where(lanes, grad_keys, merged_keys)
            merged_values = jnp.where(lanes, grad_values, merged_values)
    dkv_ref[:, :width] = (merged_keys * scale).astype(jnp.bfloat16)
    dkv_ref[:, width:] = merged_values.astype(jnp.bfloat16)

    @pl.when(step == pl.num_programs(0) - 1)
    def store():
        dq_ref[...] = sum_ref[...].astype(jnp.bfloat16)


def whole(shape):
    return pl.BlockSpec(shape, lambda step, first, last: (0,) * len(shape))


def by_rows(width):
    return pl.BlockSpec((BLOCK, width), lambda step, first, last: (step, 0))


def block_bounds(labels):
    per_block = labels.reshape(-1, BLOCK)
    least, most = per_block[:, 0], per_block[:, -1]
    first = jnp.sum(labels[None, :] < least[:, None], axis=1) // BLOCK
    last = (jnp.sum(labels[None, :] <= most[:, None], axis=1) + BLOCK - 1) // BLOCK
    return first.astype(jnp.int32), last.astype(jnp.int32)


def attend(joint, labels, bounds, heads):
    count, width = joint.shape[0], joint.shape[1] // 3
    blocks = count // BLOCK
    return pl.pallas_call(
        partial(forward_kernel, heads),
        grid_spec=pltpu.PrefetchScalarGridSpec(
            num_scalar_prefetch=2,
            grid=(blocks,),
            in_specs=[
                by_rows(width),
                whole((count, 2 * width)),
                by_rows(1),
                whole((blocks, 1, BLOCK)),
            ],
            out_specs=[by_rows(width), by_rows(heads)],
            scratch_shapes=[pltpu.VMEM((heads, blocks, BLOCK, BLOCK), jnp.float32)],
        ),
        out_shape=[
            jax.ShapeDtypeStruct((count, width), jnp.bfloat16),
            jax.ShapeDtypeStruct((count, heads), jnp.float32),
        ],
        name="attend",
    )(
        *bounds,
        joint[:, :width],
        joint[:, width:],
        labels.reshape(count, 1),
        labels.reshape(blocks, 1, BLOCK),
    )


def attend_back(joint, grad, spread, inner, labels, bounds, heads):
    count, width = joint.shape[0], joint.shape[1] // 3
    blocks = count // BLOCK

    def in_rows(value):
        return value.reshape(blocks, BLOCK, heads).transpose(0, 2, 1)

    return pl.pallas_call(
        partial(backward_kernel, heads),
        grid_spec=pltpu.PrefetchScalarGridSpec(
            num_scalar_prefetch=2,
            grid=(blocks,),
            in_specs=[
                whole((count, width)),
                by_rows(2 * width),
                whole((count, width)),
                whole((blocks, heads, BLOCK)),
                whole((blocks, heads, BLOCK)),
                by_rows(1),
                whole((blocks, 1, BLOCK)),
            ],
            out_specs=[whole((count, width)), by_rows(2 * width)],
            scratch_shapes=[pltpu.VMEM((count, width), jnp.float32)],
        ),
        out_shape=[
            jax.ShapeDtypeStruct((count, width), jnp.bfloat16),
            jax.ShapeDtypeStruct((count, 2 * width), jnp.bfloat16),
        ],
        name="attend_back",
    )(
        *bounds,
        joint[:, :width],
        joint[:, width:],
        grad,
        in_rows(spread),
        in_rows(inner),
        labels.reshape(count, 1),
        labels.reshape(blocks, 1, BLOCK),
    )


def to_heads(rows, parts, seq):
    count, width = rows.shape
    share = width // parts // seq
    split = rows.reshape(count, parts, seq, share).transpose(2, 0, 1, 3)
    moved = lax.all_to_all(split.reshape(seq, count, parts * share), "seq", 0, 0)
    return moved.reshape(seq * count, parts * share)


def to_rows(rows, parts, seq):
    count, width = rows.shape
    share = width // parts
    moved = lax.all_to_all(rows.reshape(seq, count // seq, width), "seq", 0, 0)
    split = moved.reshape(seq, count // seq, parts, share).transpose(1, 2, 0, 3)
    return split.reshape(count // seq, parts * seq * share)


def scatter_sum(value):
    near = lax.psum_scatter(value.astype(jnp.bfloat16), "grp", scatter_dimension=0, tiled=True)
    return lax.psum_scatter(near, "seq", scatter_dimension=0, tiled=True).astype(jnp.float32)


def per_device(
    tokens,
    cotangent,
    image_of_token,
    ln1_gain,
    ln1_bias,
    qkv_weight,
    q_bias,
    v_bias,
    out_weight,
    out_bias,
    ln2_gain,
    ln2_bias,
    up_weight,
    up_bias,
    down_weight,
    down_bias,
):
    f32 = jnp.float32
    bf16 = jnp.bfloat16
    width = tokens.shape[1]
    gathered = (
        lax.all_gather(ln1_gain, ("grp", "seq"), axis=0, tiled=True),
        lax.all_gather(ln1_bias, ("grp", "seq"), axis=0, tiled=True),
        lax.all_gather(qkv_weight, ("grp", "seq"), axis=0, tiled=True),
        lax.all_gather(q_bias, ("grp", "seq"), axis=0, tiled=True),
        lax.all_gather(v_bias, ("grp", "seq"), axis=0, tiled=True),
        lax.all_gather(out_weight, ("grp", "seq"), axis=0, tiled=True),
        lax.all_gather(out_bias, ("grp", "seq"), axis=0, tiled=True),
        lax.all_gather(ln2_gain, ("grp", "seq"), axis=0, tiled=True),
        lax.all_gather(ln2_bias, ("grp", "seq"), axis=0, tiled=True),
        lax.all_gather(up_weight, ("grp", "seq"), axis=0, tiled=True),
        lax.all_gather(up_bias, ("grp", "seq"), axis=0, tiled=True),
        lax.all_gather(down_weight, ("grp", "seq"), axis=0, tiled=True),
        lax.all_gather(down_bias, ("grp", "seq"), axis=0, tiled=True),
    )
    (
        gain_first,
        shift_first,
        w_joint,
        bias_query,
        bias_value,
        w_out,
        bias_out,
        gain_second,
        shift_second,
        w_up,
        bias_up,
        w_down,
        bias_down,
    ) = gathered
    inputs = tokens.astype(f32)
    normed_first = layer_norm(inputs, gain_first.astype(f32), shift_first.astype(f32)).astype(bf16)
    zeros = jnp.zeros((width,), f32)
    joint_bias = jnp.concatenate([bias_query.astype(f32), zeros, bias_value.astype(f32)])
    joint = (jnp.dot(normed_first, w_joint, preferred_element_type=f32) + joint_bias).astype(bf16)
    seq = lax.axis_size("seq")
    heads = HEADS // seq
    bounds = block_bounds(image_of_token)
    own_joint = to_heads(joint, 3, seq)
    own_attended, spread = attend(own_joint, image_of_token, bounds, heads)
    attended = to_rows(own_attended, 1, seq)
    resid = inputs + jnp.dot(attended, w_out, preferred_element_type=f32) + bias_out.astype(f32)
    normed_second = layer_norm(resid, gain_second.astype(f32), shift_second.astype(f32)).astype(
        bf16
    )
    hidden = jnp.dot(normed_second, w_up, preferred_element_type=f32) + bias_up.astype(f32)
    active = jax.nn.gelu(hidden, approximate=False).astype(bf16)
    output = (
        resid + jnp.dot(active, w_down, preferred_element_type=f32) + bias_down.astype(f32)
    ).astype(bf16)
    down_grad = rows_dot(active, cotangent).astype(bf16)
    down_bias_grad = jnp.sum(cotangent.astype(f32), axis=0)
    grad_active = dot_back(cotangent, w_down)
    _, gelu_back = jax.vjp(partial(jax.nn.gelu, approximate=False), hidden)
    grad_hidden = gelu_back(grad_active)[0].astype(bf16)
    up_grad = rows_dot(normed_second, grad_hidden).astype(bf16)
    grad_hidden, down_grad, up_grad = lax.optimization_barrier((grad_hidden, down_grad, up_grad))
    down_grad = scatter_sum(down_grad)
    up_grad = scatter_sum(up_grad)
    up_bias_grad = jnp.sum(grad_hidden.astype(f32), axis=0)
    grad_normed = dot_back(grad_hidden, w_up)
    _, second_back = jax.vjp(scaled_norm, resid, gain_second.astype(f32))
    grad_through, gain_second_grad = second_back(grad_normed)
    shift_second_grad = jnp.sum(grad_normed, axis=0)
    grad_resid = cotangent.astype(f32) + grad_through
    grad_branch = grad_resid.astype(bf16)
    out_grad = rows_dot(attended, grad_branch).astype(bf16)
    grad_branch, out_grad = lax.optimization_barrier((grad_branch, out_grad))
    out_grad = scatter_sum(out_grad)
    out_bias_grad = jnp.sum(grad_branch.astype(f32), axis=0)
    grad_attended = dot_back(grad_branch, w_out).astype(bf16)
    own_grad = to_heads(grad_attended, 1, seq)
    inner = jnp.sum(
        (own_grad.astype(f32) * own_attended.astype(f32)).reshape(own_grad.shape[0], heads, -1),
        axis=-1,
    )
    grad_q, grad_kv = attend_back(
        own_joint, own_grad, spread, inner, image_of_token, bounds, heads
    )
    grad_joint = to_rows(jnp.concatenate([grad_q, grad_kv], axis=1), 3, seq)
    joint_grad = scatter_sum(rows_dot(normed_first, grad_joint))
    column_sums = jnp.sum(grad_joint.astype(f32), axis=0)
    query_bias_grad = column_sums[:width]
    value_bias_grad = column_sums[2 * width :]
    grad_first = dot_back(grad_joint, w_joint)
    _, first_back = jax.vjp(scaled_norm, inputs, gain_first.astype(f32))
    grad_entry, gain_first_grad = first_back(grad_first)
    shift_first_grad = jnp.sum(grad_first, axis=0)
    input_grad = (grad_resid + grad_entry).astype(bf16)
    summed = (
        lax.psum_scatter(gain_first_grad, ("grp", "seq"), scatter_dimension=0, tiled=True),
        lax.psum_scatter(shift_first_grad, ("grp", "seq"), scatter_dimension=0, tiled=True),
        joint_grad,
        lax.psum_scatter(query_bias_grad, ("grp", "seq"), scatter_dimension=0, tiled=True),
        lax.psum_scatter(value_bias_grad, ("grp", "seq"), scatter_dimension=0, tiled=True),
        out_grad,
        lax.psum_scatter(out_bias_grad, ("grp", "seq"), scatter_dimension=0, tiled=True),
        lax.psum_scatter(gain_second_grad, ("grp", "seq"), scatter_dimension=0, tiled=True),
        lax.psum_scatter(shift_second_grad, ("grp", "seq"), scatter_dimension=0, tiled=True),
        up_grad,
        lax.psum_scatter(up_bias_grad, ("grp", "seq"), scatter_dimension=0, tiled=True),
        down_grad,
        lax.psum_scatter(down_bias_grad, ("grp", "seq"), scatter_dimension=0, tiled=True),
    )
    return (output, input_grad) + tuple(summed)


def solution(mesh):
    placed = (
        P(("grp", "seq"), None),
        P(("grp", "seq"), None),
        P("grp"),
        P(("grp", "seq")),
        P(("grp", "seq")),
        P(("grp", "seq"), None),
        P(("grp", "seq")),
        P(("grp", "seq")),
        P(("grp", "seq"), None),
        P(("grp", "seq")),
        P(("grp", "seq")),
        P(("grp", "seq")),
        P(("grp", "seq"), None),
        P(("grp", "seq")),
        P(("grp", "seq"), None),
        P(("grp", "seq")),
    )
    return jax.shard_map(
        per_device,
        mesh=mesh,
        in_specs=placed,
        out_specs=(
            P(("grp", "seq"), None),
            P(("grp", "seq"), None),
            P(("grp", "seq")),
            P(("grp", "seq")),
            P(("grp", "seq"), None),
            P(("grp", "seq")),
            P(("grp", "seq")),
            P(("grp", "seq"), None),
            P(("grp", "seq")),
            P(("grp", "seq")),
            P(("grp", "seq")),
            P(("grp", "seq"), None),
            P(("grp", "seq")),
            P(("grp", "seq"), None),
            P(("grp", "seq")),
        ),
        check_vma=False,
    )
```

```python
from functools import partial
import math

import jax
import jax.numpy as jnp
from jax import lax
from jax.experimental import pallas as pl
from jax.experimental.pallas import tpu as pltpu
from jax.sharding import PartitionSpec as P

HEADS = 16


EPS = 1e-06
MASKED = -1e30


def layer_norm(value, gain, shift):
    center = value - jnp.mean(value, axis=-1, keepdims=True)
    spread = jnp.mean(center * center, axis=-1, keepdims=True)
    return center * lax.rsqrt(spread + EPS) * gain + shift


def scaled_norm(value, gain):
    return layer_norm(value, gain, 0.0)


def rows_dot(left, right):
    return lax.dot_general(
        left, right, (((0,), (0,)), ((), ())), preferred_element_type=jnp.float32
    )


def dot_back(left, right):
    return lax.dot_general(
        left, right, (((1,), (1,)), ((), ())), preferred_element_type=jnp.float32
    )


BLOCK = 256


def head_lanes(shape, head, size):
    lane = lax.broadcasted_iota(jnp.int32, shape, len(shape) - 1)
    return lane // size == head


def only_head(value, head, size):
    return jnp.where(head_lanes(value.shape, head, size), value, jnp.zeros_like(value))


def forward_kernel(
    heads, first_ref, last_ref, q_ref, kv_ref, row_ref, col_ref, out_ref, lse_ref,
    s_ref, own_ref, peak_ref, total_ref, sum_ref
):
    step = pl.program_id(0)
    first = first_ref[step]
    last = last_ref[step]
    width = q_ref.shape[1]
    size = width // heads
    half = BLOCK // 2
    query = q_ref[...] * (1.0 / math.sqrt(size))
    for head in range(heads):
        own_ref[head] = only_head(query, head, size)
    peak_ref[...] = jnp.full_like(peak_ref, MASKED)
    total_ref[...] = jnp.zeros_like(total_ref)
    sum_ref[...] = jnp.zeros_like(sum_ref)
    mine = row_ref[...]

    def scores_at(at, carry):
        rows = pl.ds(pl.multiple_of(at * BLOCK, BLOCK), BLOCK)
        keys = kv_ref[rows, :width]
        same = mine == col_ref[at]
        for head in range(heads):
            scores = dot_back(own_ref[head], keys)
            scores = jnp.where(same, scores, MASKED)
            s_ref[head, at] = scores
            most = jnp.maximum(scores[:, :half], scores[:, half:])
            peak_ref[head] = jnp.maximum(peak_ref[head], most)
        return carry

    lax.fori_loop(first, last, scores_at, 0)
    peaks = [jnp.max(peak_ref[head], axis=-1, keepdims=True) for head in range(heads)]

    def sum_at(at, carry):
        rows = pl.ds(pl.multiple_of(at * BLOCK, BLOCK), BLOCK)
        values = kv_ref[rows, width:]
        result = sum_ref[...]
        for head in range(heads):
            expo = jnp.exp(s_ref[head, at] - peaks[head])
            total_ref[head] += expo[:, :half] + expo[:, half:]
            result = result + jnp.dot(
                expo.astype(jnp.bfloat16),
                only_head(values, head, size),
                preferred_element_type=jnp.float32,
            )
        sum_ref[...] = result
        return carry

    lax.fori_loop(first, last, sum_at, 0)
    merged = jnp.zeros((BLOCK, width), jnp.float32)
    for head in range(heads):
        total = jnp.sum(total_ref[head], axis=-1, keepdims=True)
        lse_ref[:, head : head + 1] = peaks[head] + jnp.log(total)
        merged = jnp.where(head_lanes(merged.shape, head, size), sum_ref[...] / total, merged)
    out_ref[...] = merged.astype(out_ref.dtype)


def backward_kernel(
    heads, first_ref, last_ref, q_ref, kv_ref, g_ref, lse_ref, delta_ref, row_ref, col_ref,
    dq_ref, dkv_ref, sum_ref, own_ref, key_sum_ref, value_sum_ref
):
    step = pl.program_id(0)
    first = first_ref[step]
    last = last_ref[step]
    width = q_ref.shape[1]
    size = width // heads
    scale = 1.0 / math.sqrt(size)

    @pl.when(step == 0)
    def clear():
        sum_ref[...] = jnp.zeros_like(sum_ref)

    scaled = kv_ref[:, :width] * scale
    for head in range(heads):
        own_ref[head] = only_head(scaled, head, size)
    key_sum_ref[...] = jnp.zeros_like(key_sum_ref)
    value_sum_ref[...] = jnp.zeros_like(value_sum_ref)
    mine = row_ref[...]

    def at_queries(at, carry):
        rows = pl.ds(pl.multiple_of(at * BLOCK, BLOCK), BLOCK)
        query = q_ref[rows, :]
        grad = g_ref[rows, :]
        values = kv_ref[:, width:]
        same = mine == col_ref[at]
        sum_keys = key_sum_ref[...]
        sum_values = value_sum_ref[...]
        sum_queries = sum_ref[rows, :]
        for head in range(heads):
            own_keys = own_ref[head]
            own_grad = only_head(grad, head, size)
            scores = jnp.where(same, dot_back(own_keys, query), MASKED)
            weights = jnp.exp(scores - lse_ref[at, head : head + 1, :])
            grad_probs = dot_back(values, own_grad)
            grad_scores = (weights * (grad_probs - delta_ref[at, head : head + 1, :])).astype(
                jnp.bfloat16
            )
            sum_values = sum_values + jnp.dot(
                weights.astype(jnp.bfloat16), own_grad, preferred_element_type=jnp.float32
            )
            sum_keys = sum_keys + jnp.dot(
                grad_scores, only_head(query, head, size), preferred_element_type=jnp.float32
            )
            sum_queries = sum_queries + rows_dot(grad_scores, own_keys)
        key_sum_ref[...] = sum_keys
        value_sum_ref[...] = sum_values
        sum_ref[rows, :] = sum_queries
        return carry

    lax.fori_loop(first, last, at_queries, 0)
    dkv_ref[:, :width] = (key_sum_ref[...] * scale).astype(jnp.bfloat16)
    dkv_ref[:, width:] = value_sum_ref[...].astype(jnp.bfloat16)

    @pl.when(step == pl.num_programs(0) - 1)
    def store():
        dq_ref[...] = sum_ref[...].astype(jnp.bfloat16)


def whole(shape):
    return pl.BlockSpec(shape, lambda step, first, last: (0,) * len(shape))


def by_rows(width):
    return pl.BlockSpec((BLOCK, width), lambda step, first, last: (step, 0))


def block_bounds(labels):
    per_block = labels.reshape(-1, BLOCK)
    least, most = per_block[:, 0], per_block[:, -1]
    first = jnp.sum(labels[None, :] < least[:, None], axis=1) // BLOCK
    last = (jnp.sum(labels[None, :] <= most[:, None], axis=1) + BLOCK - 1) // BLOCK
    return first.astype(jnp.int32), last.astype(jnp.int32)


def attend(joint, labels, bounds, heads):
    count, width = joint.shape[0], joint.shape[1] // 3
    blocks = count // BLOCK
    return pl.pallas_call(
        partial(forward_kernel, heads),
        grid_spec=pltpu.PrefetchScalarGridSpec(
            num_scalar_prefetch=2,
            grid=(blocks,),
            in_specs=[
                by_rows(width),
                whole((count, 2 * width)),
                by_rows(1),
                whole((blocks, 1, BLOCK)),
            ],
            out_specs=[by_rows(width), by_rows(heads)],
            scratch_shapes=[
                pltpu.VMEM((heads, blocks, BLOCK, BLOCK), jnp.float32),
                pltpu.VMEM((heads, BLOCK, width), jnp.bfloat16),
                pltpu.VMEM((heads, BLOCK, BLOCK // 2), jnp.float32),
                pltpu.VMEM((heads, BLOCK, BLOCK // 2), jnp.float32),
                pltpu.VMEM((BLOCK, width), jnp.float32),
            ],
        ),
        out_shape=[
            jax.ShapeDtypeStruct((count, width), jnp.bfloat16),
            jax.ShapeDtypeStruct((count, heads), jnp.float32),
        ],
        name="attend",
    )(
        *bounds,
        joint[:, :width],
        joint[:, width:],
        labels.reshape(count, 1),
        labels.reshape(blocks, 1, BLOCK),
    )


def attend_back(joint, grad, spread, inner, labels, bounds, heads):
    count, width = joint.shape[0], joint.shape[1] // 3
    blocks = count // BLOCK

    def in_rows(value):
        return value.reshape(blocks, BLOCK, heads).transpose(0, 2, 1)

    return pl.pallas_call(
        partial(backward_kernel, heads),
        grid_spec=pltpu.PrefetchScalarGridSpec(
            num_scalar_prefetch=2,
            grid=(blocks,),
            in_specs=[
                whole((count, width)),
                by_rows(2 * width),
                whole((count, width)),
                whole((blocks, heads, BLOCK)),
                whole((blocks, heads, BLOCK)),
                by_rows(1),
                whole((blocks, 1, BLOCK)),
            ],
            out_specs=[whole((count, width)), by_rows(2 * width)],
            scratch_shapes=[
                pltpu.VMEM((count, width), jnp.float32),
                pltpu.VMEM((heads, BLOCK, width), jnp.bfloat16),
                pltpu.VMEM((BLOCK, width), jnp.float32),
                pltpu.VMEM((BLOCK, width), jnp.float32),
            ],
        ),
        out_shape=[
            jax.ShapeDtypeStruct((count, width), jnp.bfloat16),
            jax.ShapeDtypeStruct((count, 2 * width), jnp.bfloat16),
        ],
        name="attend_back",
    )(
        *bounds,
        joint[:, :width],
        joint[:, width:],
        grad,
        in_rows(spread),
        in_rows(inner),
        labels.reshape(count, 1),
        labels.reshape(blocks, 1, BLOCK),
    )


def to_heads(rows, parts, seq):
    count, width = rows.shape
    share = width // parts // seq
    split = rows.reshape(count, parts, seq, share).transpose(2, 0, 1, 3)
    moved = lax.all_to_all(split.reshape(seq, count, parts * share), "seq", 0, 0)
    return moved.reshape(seq * count, parts * share)


def to_rows(rows, parts, seq):
    count, width = rows.shape
    share = width // parts
    moved = lax.all_to_all(rows.reshape(seq, count // seq, width), "seq", 0, 0)
    split = moved.reshape(seq, count // seq, parts, share).transpose(1, 2, 0, 3)
    return split.reshape(count // seq, parts * seq * share)


def scatter_sum(value):
    near = lax.psum_scatter(value.astype(jnp.bfloat16), "grp", scatter_dimension=0, tiled=True)
    return lax.psum_scatter(near, "seq", scatter_dimension=0, tiled=True).astype(jnp.float32)


def with_vectors(value, vectors):
    count = value.shape[0]
    columns = jnp.concatenate([vector.reshape(count, -1) for vector in vectors], axis=1)
    columns = jnp.pad(columns, ((0, 0), (0, 128 - columns.shape[1])))
    return jnp.concatenate([value.astype(jnp.bfloat16), columns.astype(jnp.bfloat16)], axis=1)


def split_vectors(value, width, counts):
    vectors, at = [], width
    for count in counts:
        vectors.append(value[:, at : at + count].reshape(-1))
        at += count
    return value[:, :width], vectors


def per_device(
    tokens,
    cotangent,
    image_of_token,
    ln1_gain,
    ln1_bias,
    qkv_weight,
    q_bias,
    v_bias,
    out_weight,
    out_bias,
    ln2_gain,
    ln2_bias,
    up_weight,
    up_bias,
    down_weight,
    down_bias,
):
    f32 = jnp.float32
    bf16 = jnp.bfloat16
    width = tokens.shape[1]
    everyone = ("grp", "seq")
    ratio = down_weight.shape[0] // up_weight.shape[0]
    first_pack = with_vectors(
        qkv_weight,
        (ln1_gain, ln1_bias, q_bias, v_bias, out_bias, ln2_gain, ln2_bias, down_bias, up_bias),
    )
    first_pack = lax.all_gather(first_pack, everyone, axis=0, tiled=True)
    w_joint, vectors = split_vectors(first_pack, 3 * width, (1,) * 8 + (ratio,))
    (
        gain_first,
        shift_first,
        bias_query,
        bias_value,
        bias_out,
        gain_second,
        shift_second,
        bias_down,
        bias_up,
    ) = vectors
    rows = up_weight.shape[0]
    second_pack = jnp.concatenate(
        [up_weight, out_weight]
        + [down_weight[part * rows : (part + 1) * rows] for part in range(ratio)],
        axis=1,
    )
    second_pack = lax.all_gather(second_pack, everyone, axis=0, tiled=True)
    w_up = second_pack[:, : ratio * width]
    w_out = second_pack[:, ratio * width : (ratio + 1) * width]
    w_down = second_pack[:, (ratio + 1) * width :].reshape(-1, rows, ratio, width)
    w_down = w_down.transpose(0, 2, 1, 3).reshape(ratio * width, width)
    inputs = tokens.astype(f32)
    normed_first = layer_norm(inputs, gain_first.astype(f32), shift_first.astype(f32)).astype(bf16)
    zeros = jnp.zeros((width,), f32)
    joint_bias = jnp.concatenate([bias_query.astype(f32), zeros, bias_value.astype(f32)])
    joint = (jnp.dot(normed_first, w_joint, preferred_element_type=f32) + joint_bias).astype(bf16)
    seq = lax.axis_size("seq")
    heads = HEADS // seq
    bounds = block_bounds(image_of_token)
    own_joint = to_heads(joint, 3, seq)
    own_attended, spread = attend(own_joint, image_of_token, bounds, heads)
    attended = to_rows(own_attended, 1, seq)
    resid = inputs + jnp.dot(attended, w_out, preferred_element_type=f32) + bias_out.astype(f32)
    normed_second = layer_norm(resid, gain_second.astype(f32), shift_second.astype(f32)).astype(
        bf16
    )
    hidden = jnp.dot(normed_second, w_up, preferred_element_type=f32) + bias_up.astype(f32)
    below = 0.5 * (1.0 + lax.erf(hidden * math.sqrt(0.5)))
    slope = below + hidden * (jnp.exp(-0.5 * hidden * hidden) * (1.0 / math.sqrt(2.0 * math.pi)))
    active, slope = lax.optimization_barrier(((hidden * below).astype(bf16), slope))
    down_grad = rows_dot(active, cotangent).astype(bf16)
    active, down_grad = lax.optimization_barrier((active, down_grad))
    down_grad = scatter_sum(down_grad)
    grad_hidden = (dot_back(cotangent, w_down) * slope).astype(bf16)
    up_grad = rows_dot(normed_second, grad_hidden).astype(bf16)
    grad_hidden, up_grad = lax.optimization_barrier((grad_hidden, up_grad))
    up_grad = scatter_sum(up_grad)
    output = (
        resid + jnp.dot(active, w_down, preferred_element_type=f32) + bias_down.astype(f32)
    ).astype(bf16)
    down_bias_grad = jnp.sum(cotangent.astype(f32), axis=0)
    up_bias_grad = jnp.sum(grad_hidden.astype(f32), axis=0)
    grad_normed = dot_back(grad_hidden, w_up)
    _, second_back = jax.vjp(scaled_norm, resid, gain_second.astype(f32))
    grad_through, gain_second_grad = second_back(grad_normed)
    shift_second_grad = jnp.sum(grad_normed, axis=0)
    grad_resid = cotangent.astype(f32) + grad_through
    grad_branch = grad_resid.astype(bf16)
    out_bias_grad = jnp.sum(grad_branch.astype(f32), axis=0)
    out_grad = with_vectors(
        rows_dot(attended, grad_branch),
        (out_bias_grad, gain_second_grad, shift_second_grad, down_bias_grad, up_bias_grad),
    )
    grad_branch, out_grad = lax.optimization_barrier((grad_branch, out_grad))
    out_grad, early = split_vectors(scatter_sum(out_grad), width, (1, 1, 1, 1, bias_up.shape[0] // width))
    out_bias_grad, gain_second_grad, shift_second_grad, down_bias_grad, up_bias_grad = early
    grad_attended = dot_back(grad_branch, w_out).astype(bf16)
    own_grad = to_heads(grad_attended, 1, seq)
    inner = jnp.sum(
        (own_grad.astype(f32) * own_attended.astype(f32)).reshape(own_grad.shape[0], heads, -1),
        axis=-1,
    )
    grad_q, grad_kv = attend_back(
        own_joint, own_grad, spread, inner, image_of_token, bounds, heads
    )
    grad_joint = to_rows(jnp.concatenate([grad_q, grad_kv], axis=1), 3, seq)
    column_sums = jnp.sum(grad_joint.astype(f32), axis=0)
    query_bias_grad = column_sums[:width]
    value_bias_grad = column_sums[2 * width :]
    grad_first = dot_back(grad_joint, w_joint)
    _, first_back = jax.vjp(scaled_norm, inputs, gain_first.astype(f32))
    grad_entry, gain_first_grad = first_back(grad_first)
    shift_first_grad = jnp.sum(grad_first, axis=0)
    input_grad = (grad_resid + grad_entry).astype(bf16)
    joint_grad = with_vectors(
        rows_dot(normed_first, grad_joint),
        (gain_first_grad, shift_first_grad, query_bias_grad, value_bias_grad),
    )
    joint_grad, late = split_vectors(scatter_sum(joint_grad), 3 * width, (1, 1, 1, 1))
    gain_first_grad, shift_first_grad, query_bias_grad, value_bias_grad = late
    return (
        output,
        input_grad,
        gain_first_grad,
        shift_first_grad,
        joint_grad,
        query_bias_grad,
        value_bias_grad,
        out_grad,
        out_bias_grad,
        gain_second_grad,
        shift_second_grad,
        up_grad,
        up_bias_grad,
        down_grad,
        down_bias_grad,
    )


def solution(mesh):
    placed = (
        P(("grp", "seq"), None),
        P(("grp", "seq"), None),
        P("grp"),
        P(("grp", "seq")),
        P(("grp", "seq")),
        P(("grp", "seq"), None),
        P(("grp", "seq")),
        P(("grp", "seq")),
        P(("grp", "seq"), None),
        P(("grp", "seq")),
        P(("grp", "seq")),
        P(("grp", "seq")),
        P(("grp", "seq"), None),
        P(("grp", "seq")),
        P(("grp", "seq"), None),
        P(("grp", "seq")),
    )
    return jax.shard_map(
        per_device,
        mesh=mesh,
        in_specs=placed,
        out_specs=(
            P(("grp", "seq"), None),
            P(("grp", "seq"), None),
            P(("grp", "seq")),
            P(("grp", "seq")),
            P(("grp", "seq"), None),
            P(("grp", "seq")),
            P(("grp", "seq")),
            P(("grp", "seq"), None),
            P(("grp", "seq")),
            P(("grp", "seq")),
            P(("grp", "seq")),
            P(("grp", "seq"), None),
            P(("grp", "seq")),
            P(("grp", "seq"), None),
            P(("grp", "seq")),
        ),
        check_vma=False,
    )
```
